32 devices in a mesh: gz: 2 (over x), gy: 4 (over y, core), gx: 4 (over z).
Axes of the slice: x: 2, y: 2, z: 4, core: 2. Of those that a mesh axis runs over, the one named last changes fastest.
Arguments:
- pressure: float32 [8, 512, 512], P('gz', 'gy', 'gx'), may hold values from -6 to 6
- light: float32 [4, 3], replicated, may hold values from -4 to 4
- palette: float32 [3, 2], replicated, may hold values from -4 to 4
- rate: float32 [4], replicated, may hold values from 0.0625 to 0.375
- shear: int32 [4, 8, 2], replicated, may hold values from 0 to 8
- offset: int32 [4, 2, 2], replicated, may hold values from 0 to 31
- order: int32 [4, 2], replicated, may hold values from 0 to 1, each once within a row
Outputs:
- picture: float32 [4, 4, 2, 256, 512], P(None, None, 'gz', 'gy', 'gx')
The draws below stay inside these ranges and needn't reach their ends.
Inputs may be any that keep to these rules, and one draw needn't show every extreme that they name: `order`: each row is a permutation of 0 to 1.
All inputs are finite; a program needn't handle non-finite values.
Results may differ from the reference program's by a relative error of at most 0.00005.
Values sent between devices are 32-bit elements; how exact they have to be, the bound alone decides.
A program may use at most 64 MiB of HBM per device.

```python
import math
import jax
import jax.numpy as jnp
from jax import lax

BZ = 4
VIEWS = 4
SHEAR = 8
REACH = 32
NBRICK = 2
NZ = 8
NY = 512
NX = 512
ROWS = 64
N_GY = 4


def draw_shear(key, part):
    drawn = jax.random.randint(jax.random.fold_in(key, 11), (VIEWS, NZ, 2), 0, SHEAR + 1)
    picked = jax.random.randint(jax.random.fold_in(key, 12), (VIEWS,), 0, NZ)
    marked = (jnp.arange(NZ, dtype=jnp.int32)[None, :] == picked[:, None])[:, :, None]
    return jnp.where(marked, SHEAR, drawn).astype(jnp.int32)


def draw_offset(key, part):
    drawn = jax.random.randint(jax.random.fold_in(key, 21), (VIEWS, NBRICK, 2), 0, REACH)
    picked = jax.random.randint(jax.random.fold_in(key, 22), (VIEWS,), 0, NBRICK)
    marked = (jnp.arange(NBRICK, dtype=jnp.int32)[None, :] == picked[:, None])[:, :, None]
    return jnp.where(marked, REACH - 1, drawn).astype(jnp.int32)


def block_levels(own_key, shape, split, low, high):
    def one(axis_at, shards_of):
        steps = jax.random.uniform(jax.random.fold_in(jax.random.fold_in(own_key, 6), axis_at), (shards_of,), jnp.float32, low / len(split), high / len(split))
        return jnp.repeat(jnp.exp(steps), shape[axis_at] // shards_of).reshape((-1,) + (1,) * (len(shape) - axis_at - 1))

    factor_of = one(*split[0])
    for cut in split[1:]:
        factor_of = factor_of * one(*cut)
    return factor_of


def bell_draw(stream_key, extent, spread, limit, split=(), kind=jnp.bfloat16):
    gain = block_levels(stream_key, extent, split, -0.22, 0.18) if split else 1.0
    result = jax.random.normal(stream_key, extent, jnp.float32) * spread * gain
    return jnp.minimum(jnp.maximum(result, -limit), limit).astype(kind)


def setup_inputs(seed: int = 0) -> dict:
    seeds = jax.random.split(jax.random.key(seed), 8)
    pressure = bell_draw(seeds[0], (NZ, NY, NX), 1.0, 6.0, ((0, 2), (1, 4), (2, 4)), jnp.float32)
    light = bell_draw(seeds[1], (VIEWS, 3), 1.0, 4.0, (), jnp.float32)
    palette = bell_draw(seeds[2], (3, 2), 1.0, 4.0, (), jnp.float32)
    rate = jnp.clip(jnp.exp(jax.random.uniform(seeds[3], (VIEWS,), jnp.float32, math.log(0.0625), math.log(0.375))), 0.0625, 0.375)
    shear = draw_shear(jax.random.fold_in(seeds[7], 71), 0)
    offset = draw_offset(jax.random.fold_in(seeds[7], 71), 0)
    order = jax.vmap(lambda own: jax.random.permutation(own, NBRICK))(jax.random.split(seeds[6], VIEWS)).reshape((VIEWS, NBRICK)).astype(jnp.int32)
    return dict(pressure=pressure, light=light, palette=palette, rate=rate, shear=shear, offset=offset, order=order)


def surface_terms(slab):
    inner = slab[1:-1, 1:-1, 1:-1]
    grad_depth = 0.5 * (slab[2:, 1:-1, 1:-1] - slab[:-2, 1:-1, 1:-1])
    grad_rows = 0.5 * (slab[1:-1, 2:, 1:-1] - slab[1:-1, :-2, 1:-1])
    grad_cols = 0.5 * (slab[1:-1, 1:-1, 2:] - slab[1:-1, 1:-1, :-2])
    factor = lax.rsqrt(grad_depth * grad_depth + grad_rows * grad_rows + grad_cols * grad_cols + 1.0)
    return (inner, (grad_depth * factor, grad_rows * factor, grad_cols * factor))

def render_layers(inner, normals, shifts, light, palette, rate, rows, cols):
    lengths = jnp.sqrt(lax.optimization_barrier(jnp.sum(light * light, axis=1, keepdims=True)) + 1.0)
    towards = light / lengths
    offsets = palette[:, 0][:, None, None]
    slopes = palette[:, 1][:, None, None]
    layers = []
    for view in range(light.shape[0]):

        def advance(carry, items):
            color, depth = carry
            value_slab, normal_depth, normal_rows, normal_cols, moved = items
            start = (SHEAR - moved[0], SHEAR - moved[1])
            value = lax.dynamic_slice(value_slab, start, (rows, cols))
            dot = lax.dynamic_slice(normal_depth, start, (rows, cols)) * towards[view, 0] + lax.dynamic_slice(normal_rows, start, (rows, cols)) * towards[view, 1] + lax.dynamic_slice(normal_cols, start, (rows, cols)) * towards[view, 2]
            shade = 0.25 + 0.75 * dot * dot
            density = rate[view] * (1.0 + jnp.tanh(value))
            alpha = 1.0 - jnp.exp(-density)
            weight = alpha * jnp.exp(-depth)
            hues = jax.nn.sigmoid(offsets + slopes * value[None]) * shade[None]
            return ((color + hues * weight[None], depth + density), None)
        start_carry = (jnp.zeros((3, rows, cols), jnp.float32), jnp.zeros((rows, cols), jnp.float32))
        (color, depth), _ = lax.scan(advance, start_carry, (inner, normals[0], normals[1], normals[2], shifts[view]))
        layers.append(jnp.concatenate([color, depth[None]], axis=0))
    return jnp.stack(layers)

def precedence(order):
    bricks = order.shape[1]
    onehot = (order[:, :, None] == jnp.arange(bricks, dtype=jnp.int32)[None, None, :]).astype(jnp.float32)
    ranks = lax.optimization_barrier(jnp.sum(onehot * jnp.arange(bricks, dtype=jnp.float32)[None, :, None], axis=1))
    return (ranks[:, None, :] < ranks[:, :, None]).astype(jnp.float32)

def place(layer, moved):
    padded = jnp.pad(layer, ((0, 0), (REACH, 0), (REACH, 0)))
    zero = jnp.zeros((), jnp.int32)
    return lax.dynamic_slice(padded, (zero, REACH - moved[0], REACH - moved[1]), layer.shape)

def reference(pressure, light, palette, rate, shear, offset, order):
    margin = SHEAR + 1
    rows = pressure.shape[1]
    cols = pressure.shape[2]
    padded = jnp.pad(pressure, ((1, 1), (margin, margin), (margin, margin)))

    def one_brick(brick):
        zero = jnp.zeros((), jnp.int32)
        slab = lax.dynamic_slice(padded, (brick * BZ, zero, zero), (BZ + 2, rows + 2 * margin, cols + 2 * margin))
        inner, normals = surface_terms(slab)
        shifts = lax.dynamic_slice(shear, (zero, brick * BZ, zero), (VIEWS, BZ, 2))
        layers = render_layers(inner, normals, shifts, light, palette, rate, rows, cols)
        moved = lax.dynamic_index_in_dim(offset, brick, 1, keepdims=False)
        return jnp.stack([place(layers[view], moved[view]) for view in range(VIEWS)])
    stacked = lax.map(one_brick, jnp.arange(NBRICK, dtype=jnp.int32))
    ranking = precedence(order)
    depths = stacked[:, :, 3]
    cover = jnp.einsum('vbc,cvyx->bvyx', ranking, depths, precision=lax.Precision.HIGHEST)
    colors = lax.optimization_barrier(jnp.sum(stacked[:, :, :3] * jnp.exp(-cover)[:, :, None], axis=0))
    opacity = 1.0 - jnp.exp(-lax.optimization_barrier(jnp.sum(depths, axis=0)))
    image = jnp.concatenate([colors, opacity[:, None]], axis=1)
    image = image.reshape(VIEWS, 4, N_GY, NBRICK, ROWS, NX)
    image = jnp.transpose(image, (0, 1, 3, 2, 4, 5))
    return image.reshape(VIEWS, 4, NBRICK, N_GY * ROWS, NX)
```

```python
import functools
import math

import jax
import jax.numpy as jnp
from jax import lax
from jax.experimental import pallas as pl
from jax.experimental.pallas import tpu as pltpu
from jax.sharding import PartitionSpec as P

VIEWS = 4
SHEAR = 8
REACH = 32
HALO = SHEAR + REACH
SUB = 8
LANES = 128
MESH = pl.DeviceIdType.MESH


def padded(cells, sides, width):
    for axis, dim in sides:
        count = lax.axis_size(axis)
        ends = count - 1
        head = lax.slice_in_dim(cells, 0, width, axis=dim)
        tail = lax.slice_in_dim(cells, cells.shape[dim] - width, cells.shape[dim], axis=dim)
        cells = jnp.concatenate(
            [
                lax.ppermute(tail, axis, [(i, (i + 1) % count) for i in range(ends)]),
                cells,
                lax.ppermute(head, axis, [((i + 1) % count, i) for i in range(ends)]),
            ],
            axis=dim,
        )
    return cells


def shifted(value, axis, steps):
    count = lax.axis_size(axis)
    first, last = (max(0, -steps), min(count, count - steps))
    return lax.ppermute(value, axis, [(source, source + steps) for source in range(first, last)])


def surface_terms(slab):
    inner = slab[1:-1, 1:-1, 1:-1]
    grad_depth = 0.5 * (slab[2:, 1:-1, 1:-1] - slab[:-2, 1:-1, 1:-1])
    grad_rows = 0.5 * (slab[1:-1, 2:, 1:-1] - slab[1:-1, :-2, 1:-1])
    grad_cols = 0.5 * (slab[1:-1, 1:-1, 2:] - slab[1:-1, 1:-1, :-2])
    factor = lax.rsqrt(
        grad_depth * grad_depth + grad_rows * grad_rows + grad_cols * grad_cols + 1.0
    )
    return (inner, (grad_depth * factor, grad_rows * factor, grad_cols * factor))


def render_layers(inner, normals, shifts, light, palette, rate, rows, cols):
    lengths = jnp.sqrt(jnp.sum(light * light, axis=1, keepdims=True) + 1.0)
    towards = light / lengths
    offsets = palette[:, 0][:, None, None]
    slopes = palette[:, 1][:, None, None]
    layers = []
    for view in range(light.shape[0]):

        def advance(carry, items):
            color, depth = carry
            value_slab, normal_depth, normal_rows, normal_cols, moved = items
            start = (SHEAR - moved[0], SHEAR - moved[1])
            value = lax.dynamic_slice(value_slab, start, (rows, cols))
            dot = (
                lax.dynamic_slice(normal_depth, start, (rows, cols)) * towards[view, 0]
                + lax.dynamic_slice(normal_rows, start, (rows, cols)) * towards[view, 1]
                + lax.dynamic_slice(normal_cols, start, (rows, cols)) * towards[view, 2]
            )
            shade = 0.25 + 0.75 * dot * dot
            density = rate[view] * (1.0 + jnp.tanh(value))
            alpha = 1.0 - jnp.exp(-density)
            weight = alpha * jnp.exp(-depth)
            hues = jax.nn.sigmoid(offsets + slopes * value[None]) * shade[None]
            return ((color + hues * weight[None], depth + density), None)

        start_carry = (
            jnp.zeros((3, rows, cols), jnp.float32),
            jnp.zeros((rows, cols), jnp.float32),
        )
        (color, depth), _ = lax.scan(
            advance, start_carry, (inner, normals[0], normals[1], normals[2], shifts[view])
        )
        layers.append(jnp.concatenate([color, depth[None]], axis=0))
    return jnp.stack(layers)


def precedence(order):
    bricks = order.shape[1]
    onehot = (order[:, :, None] == jnp.arange(bricks, dtype=jnp.int32)[None, None, :]).astype(
        jnp.float32
    )
    ranks = jnp.sum(onehot * jnp.arange(bricks, dtype=jnp.float32)[None, :, None], axis=1)
    return (ranks[:, None, :] < ranks[:, :, None]).astype(jnp.float32)


def many_bricks(pressure, light, palette, rate, shear, offset, order):
    depth_cells, rows, cols = pressure.shape
    brick = lax.axis_index("gz")
    zero = jnp.zeros((), jnp.int32)
    widened = padded(pressure, (("gy", 1), ("gx", 2)), SHEAR + 1)
    slab = padded(widened, (("gz", 0),), 1)
    inner, normals = surface_terms(slab)
    shifts = lax.dynamic_slice(shear, (zero, brick * depth_cells, zero), (VIEWS, depth_cells, 2))
    layers = render_layers(inner, normals, shifts, light, palette, rate, rows, cols)
    moved = lax.dynamic_index_in_dim(offset, brick, 1, keepdims=False)
    blank = jnp.zeros((4, rows + REACH, cols + REACH), jnp.float32)
    canvas = jnp.stack(
        [
            lax.dynamic_update_slice(blank, layers[view], (zero, moved[view, 0], moved[view, 1]))
            for view in range(VIEWS)
        ]
    )
    own_tile = canvas[:, :, :rows, :cols]
    from_above = shifted(canvas[:, :, rows:, :cols], "gy", 1)
    from_left = shifted(canvas[:, :, :rows, cols:], "gx", 1)
    from_diagonal = shifted(canvas[:, :, rows:, cols:], ("gy", "gx"), lax.axis_size("gx") + 1)
    from_diagonal = from_diagonal * (lax.axis_index("gx") > 0).astype(jnp.float32)
    own_tile = own_tile.at[:, :, :REACH, :].add(from_above)
    own_tile = own_tile.at[:, :, :, :REACH].add(from_left)
    own_tile = own_tile.at[:, :, :REACH, :REACH].add(from_diagonal)
    ranking = precedence(order)
    pieces = lax.all_to_all(own_tile[None], "gz", split_axis=3, concat_axis=0, tiled=True)
    depths = pieces[:, :, 3]
    cover = jnp.einsum("vbc,cvyx->bvyx", ranking, depths, precision=lax.Precision.HIGHEST)
    colors = jnp.sum(pieces[:, :, :3] * jnp.exp(-cover)[:, :, None], axis=0)
    opacity = 1.0 - jnp.exp(-jnp.sum(depths, axis=0))
    image = jnp.concatenate([colors, opacity[:, None]], axis=1)
    return image[:, :, None]


def gather_cells(dims, p_ref, m_ref, l_ref, r_ref, lpk, rpk, sends, arrivals):
    ny, nx, bz, rows = dims
    strip = rows // 2
    tall = HALO + strip + SUB
    z, y, x = lax.axis_index("gz"), lax.axis_index("gy"), lax.axis_index("gx")
    depth = 2 * bz

    m_ref[0] = jnp.zeros((tall, LANES), jnp.float32)
    m_ref[depth + 1] = jnp.zeros((tall, LANES), jnp.float32)
    m_ref[:, :HALO] = jnp.zeros((depth + 2, HALO, LANES), jnp.float32)
    m_ref[:, HALO + strip :] = jnp.zeros((depth + 2, SUB, LANES), jnp.float32)
    l_ref[...] = jnp.zeros(l_ref.shape, jnp.float32)
    r_ref[...] = jnp.zeros(r_ref.shape, jnp.float32)

    has_up, has_down = y > 0, y < ny - 1
    has_left, has_right = x > 0, x < nx - 1
    cross = y + 2 * z - 1
    has_cross = jnp.logical_and(cross >= 0, cross < ny)
    always = y >= 0
    partners = (
        (always, (1 - z, y, x)),
        (has_up, (z, y - 1, x)),
        (has_down, (z, y + 1, x)),
        (has_cross, (1 - z, cross, x)),
        (has_left, (z, y, x - 1)),
        (has_right, (z, y, x + 1)),
    )
    barrier = pltpu.get_barrier_semaphore()
    for there, who in partners:

        @pl.when(there)
        def _():
            pl.semaphore_signal(barrier, inc=1, device_id=who, device_id_type=MESH)

    count = 1
    for there, _ in partners[1:]:
        count = count + there.astype(jnp.int32)
    pl.semaphore_wait(barrier, count)

    def remote(src, dst, slot, arrival, who):
        return pltpu.make_async_remote_copy(
            src_ref=src,
            dst_ref=dst,
            send_sem=sends.at[slot],
            recv_sem=arrivals.at[arrival],
            device_id=who,
            device_id_type=MESH,
        )

    def planes(brick):
        return pl.ds(1 + brick * bz, bz)

    def copies(brick):
        if brick == 0:
            main = remote(
                p_ref.at[:, strip - HALO :],
                m_ref.at[planes(0), : HALO + strip],
                0, 0, (1 - z, y, x),
            )
        else:
            main = remote(
                p_ref.at[:, : strip + SUB],
                m_ref.at[planes(1), HALO:],
                0, 0, (1 - z, y, x),
            )
        down = remote(
            p_ref.at[:, rows - HALO :], m_ref.at[planes(brick), :HALO],
            1, 1 + brick, (0, y + 1, x),
        )
        up = remote(
            p_ref.at[:, :SUB], m_ref.at[planes(brick), HALO + strip :],
            2, 1 + brick, (1, y - 1, x),
        )
        return main, down, up

    for brick in range(2):

        @pl.when(z == brick)
        def _():
            main, down, up = copies(brick)
            main.start()

            @pl.when(has_down)
            def _():
                down.start()

            @pl.when(has_up)
            def _():
                up.start()

            if brick == 0:
                m_ref[planes(0), HALO:] = p_ref[:, : strip + SUB]
            else:
                m_ref[planes(1), : HALO + strip] = p_ref[:, strip - HALO :]

    for brick in range(2):

        @pl.when(z == brick)
        def _():
            main, down, up = copies(brick)
            other_main, _, _ = copies(1 - brick)
            other_main.wait_recv()
            for source in range(2):
                _, from_up, from_down = copies(source)
                if brick == 0:

                    @pl.when(has_up)
                    def _():
                        from_up.wait_recv()
                else:

                    @pl.when(has_down)
                    def _():
                        from_down.wait_recv()

    lane = lax.broadcasted_iota(jnp.int32, (tall, LANES), 1)
    per = LANES // HALO
    first_lane = LANES - HALO
    ends = jnp.zeros((tall, LANES), jnp.float32)
    for group in range(l_ref.shape[0]):
        packed = jnp.zeros((tall, LANES), jnp.float32)
        for j in range(per):
            k = group * per + j
            if k < depth:
                cells = m_ref[1 + k]
                moved = pltpu.roll(cells, (j * HALO - first_lane) % LANES, 1)
                packed = jnp.where(lane >= j * HALO, moved, packed)
                ends = jnp.where(lane == k, pltpu.roll(cells, k, 1) if k else cells, ends)
        lpk[group] = packed
    rpk[...] = ends

    rightward = remote(lpk, l_ref, 3, 3, (z, y, x + 1))
    leftward = remote(rpk, r_ref, 4, 4, (z, y, x - 1))

    @pl.when(has_right)
    def _():
        rightward.start()

    @pl.when(has_left)
    def _():
        leftward.start()
        rightward.wait_recv()

    @pl.when(has_right)
    def _():
        leftward.wait_recv()

    for brick in range(2):

        @pl.when(z == brick)
        def _():
            main, down, up = copies(brick)
            main.wait_send()

            @pl.when(has_down)
            def _():
                down.wait_send()

            @pl.when(has_up)
            def _():
                up.wait_send()

    @pl.when(has_right)
    def _():
        rightward.wait_send()

    @pl.when(has_left)
    def _():
        leftward.wait_send()


def render_strip(
    dims, light, palette, rate, shear, offset, order, m_ref, l_ref, r_ref, out_ref, h_ref, dm, dh
):
    ny, nx, bz, rows = dims
    strip = rows // 2
    tall = HALO + strip + SUB
    depth = 2 * bz
    per = LANES // HALO
    first_lane = LANES - HALO
    z, y, x = lax.axis_index("gz"), lax.axis_index("gy"), lax.axis_index("gx")

    h_ref[0] = jnp.zeros((tall, LANES), jnp.float32)
    h_ref[depth + 1] = jnp.zeros((tall, LANES), jnp.float32)
    for k in range(depth):
        shift = (first_lane - (k % per) * HALO) % LANES
        h_ref[1 + k] = pltpu.roll(l_ref[k // per], shift, 1)

    towards = []
    for w in range(VIEWS):
        a, b, c = light[w, 0], light[w, 1], light[w, 2]
        inverse = lax.rsqrt(jnp.full((SUB, LANES), a * a + b * b + c * c + 1.0, jnp.float32))
        towards.append((a * inverse, b * inverse, c * inverse))

    lane = lax.broadcasted_iota(jnp.int32, (SUB, LANES), 1)
    last = lane == LANES - 1
    first = lane == 0

    def slopes(k, carry):
        for i in range((HALO + strip) // SUB):
            top = i * SUB
            here = m_ref[k + 1, top + 1 : top + 1 + SUB]
            side = h_ref[k + 1, top + 1 : top + 1 + SUB]
            beyond = pltpu.roll(r_ref[top + 1 : top + 1 + SUB], LANES - 1 - k, 1)
            here_r, here_l = pltpu.roll(here, LANES - 1, 1), pltpu.roll(here, 1, 1)
            side_r, side_l = pltpu.roll(side, LANES - 1, 1), pltpu.roll(side, 1, 1)
            for ref, cols, dots in (
                (m_ref, jnp.where(last, beyond, here_r) - jnp.where(first, side_l, here_l), dm),
                (h_ref, jnp.where(last, here_r, side_r) - side_l, dh),
            ):
                deep = ref[k + 2, top + 1 : top + 1 + SUB] - ref[k, top + 1 : top + 1 + SUB]
                down = ref[k + 1, top + 2 : top + 2 + SUB] - ref[k + 1, top : top + SUB]
                half = 0.5 * lax.rsqrt(0.25 * (deep * deep + down * down + cols * cols) + 1.0)
                deep, down, cols = deep * half, down * half, cols * half
                for w in range(VIEWS):
                    a, b, c = towards[w]
                    dots[w, k, top : top + SUB] = deep * a + down * b + cols * c
        return carry

    lax.fori_loop(0, depth, slopes, 0)

    tile = 32
    base_row = y * rows + z * strip
    base_col = x * LANES
    lanes = lax.broadcasted_iota(jnp.int32, (tile, LANES), 1)
    rows_at = lax.broadcasted_iota(jnp.int32, (tile, LANES), 0)
    bias = [0.5 * palette[c, 0] for c in range(3)]
    gain = [0.5 * palette[c, 1] for c in range(3)]

    def view_part(step, carry):
        w = step // (strip // tile)
        top = (step % (strip // tile)) * tile
        through = jnp.ones((tile, LANES), jnp.float32)
        ambient = jnp.zeros((tile, LANES), jnp.float32)
        colors = [jnp.zeros((tile, LANES), jnp.float32) for _ in range(3)]
        rate2 = rate[w] * (-math.log2(math.e))
        for place in range(2):
            brick = order[w, place]
            off_r, off_c = offset[w, brick, 0], offset[w, brick, 1]
            inside = jnp.logical_and(
                rows_at >= off_r - base_row - top, lanes >= off_c - base_col
            )
            fall = jnp.where(inside, rate2, 0.0)
            for j in range(bz):
                k = brick * bz + j
                sr = off_r + shear[w, k, 0]
                sc = off_c + shear[w, k, 1]
                at = HALO + top - sr
                wrap = lanes >= LANES - sc
                value = jnp.where(
                    wrap, h_ref[k + 1, pl.ds(at, tile)], m_ref[k + 1, pl.ds(at, tile)]
                )
                dot = jnp.where(wrap, dh[w, k, pl.ds(at - 1, tile)], dm[w, k, pl.ds(at - 1, tile)])
                value = pltpu.roll(value, sc, 1)
                dot = pltpu.roll(dot, sc, 1)
                kept = jnp.exp2(fall * (1.0 + jnp.tanh(value)))
                weight = (0.125 + 0.375 * dot * dot) * ((1.0 - kept) * through)
                through = through * kept
                ambient = ambient + weight
                for c in range(3):
                    colors[c] = colors[c] + weight * jnp.tanh(bias[c] + gain[c] * value)
        for c in range(3):
            out_ref[w, c, pl.ds(top, tile)] = ambient + colors[c]
        out_ref[w, 3, pl.ds(top, tile)] = 1.0 - through
        return carry

    lax.fori_loop(0, VIEWS * (strip // tile), view_part, 0)


def two_bricks(mesh, pressure, light, palette, rate, shear, offset, order):
    bz, rows, cols = pressure.shape
    dims = (mesh.shape["gy"], mesh.shape["gx"], bz, rows)
    strip = rows // 2
    tall = HALO + strip + SUB
    depth = 2 * bz
    groups = -(-depth // (LANES // HALO))
    vmem = pl.BlockSpec(memory_space=pltpu.VMEM)
    smem = pl.BlockSpec(memory_space=pltpu.SMEM)
    f32 = jnp.float32
    cells, left, right = pl.pallas_call(
        functools.partial(gather_cells, dims),
        out_shape=(
            jax.ShapeDtypeStruct((depth + 2, tall, LANES), f32),
            jax.ShapeDtypeStruct((groups, tall, LANES), f32),
            jax.ShapeDtypeStruct((tall, LANES), f32),
        ),
        in_specs=[vmem],
        out_specs=(vmem, vmem, vmem),
        scratch_shapes=[
            pltpu.VMEM((groups, tall, LANES), f32),
            pltpu.VMEM((tall, LANES), f32),
            pltpu.SemaphoreType.DMA((5,)),
            pltpu.SemaphoreType.DMA((5,)),
        ],
        compiler_params=pltpu.CompilerParams(collective_id=0, has_side_effects=True),
        name="gather_cells",
    )(pressure)
    image = pl.pallas_call(
        functools.partial(render_strip, dims),
        out_shape=jax.ShapeDtypeStruct((VIEWS, 4, strip, LANES), f32),
        in_specs=[smem] * 6 + [vmem] * 3,
        out_specs=vmem,
        scratch_shapes=[
            pltpu.VMEM((depth + 2, tall, LANES), f32),
            pltpu.VMEM((VIEWS, depth, HALO + strip, LANES), f32),
            pltpu.VMEM((VIEWS, depth, HALO + strip, LANES), f32),
        ],
        name="render_strip",
    )(light, palette, rate, shear, offset, order, cells, left, right)
    return image[:, :, None]


def on_device(mesh, pressure, *rest):
    bz, rows, cols = pressure.shape
    if mesh.shape["gz"] == 2 and cols == LANES and rows % 64 == 0 and rows // 2 >= HALO:
        return two_bricks(mesh, pressure, *rest)
    return many_bricks(pressure, *rest)


def solution(mesh):
    return jax.shard_map(
        functools.partial(on_device, mesh),
        mesh=mesh,
        in_specs=(P("gz", "gy", "gx"), P(), P(), P(), P(), P(), P()),
        out_specs=P(None, None, "gz", "gy", "gx"),
        check_vma=False,
    )
```

```python
import functools
import math

import jax
import jax.numpy as jnp
from jax import lax
from jax.experimental import pallas as pl
from jax.experimental.pallas import tpu as pltpu
from jax.sharding import PartitionSpec as P

VIEWS = 4
SHEAR = 8
REACH = 32
HALO = SHEAR + REACH
SUB = 8
LANES = 128
MESH = pl.DeviceIdType.MESH


def padded(cells, sides, width):
    for axis, dim in sides:
        count = lax.axis_size(axis)
        ends = count - 1
        head = lax.slice_in_dim(cells, 0, width, axis=dim)
        tail = lax.slice_in_dim(cells, cells.shape[dim] - width, cells.shape[dim], axis=dim)
        cells = jnp.concatenate(
            [
                lax.ppermute(tail, axis, [(i, (i + 1) % count) for i in range(ends)]),
                cells,
                lax.ppermute(head, axis, [((i + 1) % count, i) for i in range(ends)]),
            ],
            axis=dim,
        )
    return cells


def shifted(value, axis, steps):
    count = lax.axis_size(axis)
    first, last = (max(0, -steps), min(count, count - steps))
    return lax.ppermute(value, axis, [(source, source + steps) for source in range(first, last)])


def surface_terms(slab):
    inner = slab[1:-1, 1:-1, 1:-1]
    grad_depth = 0.5 * (slab[2:, 1:-1, 1:-1] - slab[:-2, 1:-1, 1:-1])
    grad_rows = 0.5 * (slab[1:-1, 2:, 1:-1] - slab[1:-1, :-2, 1:-1])
    grad_cols = 0.5 * (slab[1:-1, 1:-1, 2:] - slab[1:-1, 1:-1, :-2])
    factor = lax.rsqrt(
        grad_depth * grad_depth + grad_rows * grad_rows + grad_cols * grad_cols + 1.0
    )
    return (inner, (grad_depth * factor, grad_rows * factor, grad_cols * factor))


def render_layers(inner, normals, shifts, light, palette, rate, rows, cols):
    lengths = jnp.sqrt(jnp.sum(light * light, axis=1, keepdims=True) + 1.0)
    towards = light / lengths
    offsets = palette[:, 0][:, None, None]
    slopes = palette[:, 1][:, None, None]
    layers = []
    for view in range(light.shape[0]):

        def advance(carry, items):
            color, depth = carry
            value_slab, normal_depth, normal_rows, normal_cols, moved = items
            start = (SHEAR - moved[0], SHEAR - moved[1])
            value = lax.dynamic_slice(value_slab, start, (rows, cols))
            dot = (
                lax.dynamic_slice(normal_depth, start, (rows, cols)) * towards[view, 0]
                + lax.dynamic_slice(normal_rows, start, (rows, cols)) * towards[view, 1]
                + lax.dynamic_slice(normal_cols, start, (rows, cols)) * towards[view, 2]
            )
            shade = 0.25 + 0.75 * dot * dot
            density = rate[view] * (1.0 + jnp.tanh(value))
            alpha = 1.0 - jnp.exp(-density)
            weight = alpha * jnp.exp(-depth)
            hues = jax.nn.sigmoid(offsets + slopes * value[None]) * shade[None]
            return ((color + hues * weight[None], depth + density), None)

        start_carry = (
            jnp.zeros((3, rows, cols), jnp.float32),
            jnp.zeros((rows, cols), jnp.float32),
        )
        (color, depth), _ = lax.scan(
            advance, start_carry, (inner, normals[0], normals[1], normals[2], shifts[view])
        )
        layers.append(jnp.concatenate([color, depth[None]], axis=0))
    return jnp.stack(layers)


def precedence(order):
    bricks = order.shape[1]
    onehot = (order[:, :, None] == jnp.arange(bricks, dtype=jnp.int32)[None, None, :]).astype(
        jnp.float32
    )
    ranks = jnp.sum(onehot * jnp.arange(bricks, dtype=jnp.float32)[None, :, None], axis=1)
    return (ranks[:, None, :] < ranks[:, :, None]).astype(jnp.float32)


def many_bricks(pressure, light, palette, rate, shear, offset, order):
    depth_cells, rows, cols = pressure.shape
    brick = lax.axis_index("gz")
    zero = jnp.zeros((), jnp.int32)
    widened = padded(pressure, (("gy", 1), ("gx", 2)), SHEAR + 1)
    slab = padded(widened, (("gz", 0),), 1)
    inner, normals = surface_terms(slab)
    shifts = lax.dynamic_slice(shear, (zero, brick * depth_cells, zero), (VIEWS, depth_cells, 2))
    layers = render_layers(inner, normals, shifts, light, palette, rate, rows, cols)
    moved = lax.dynamic_index_in_dim(offset, brick, 1, keepdims=False)
    blank = jnp.zeros((4, rows + REACH, cols + REACH), jnp.float32)
    canvas = jnp.stack(
        [
            lax.dynamic_update_slice(blank, layers[view], (zero, moved[view, 0], moved[view, 1]))
            for view in range(VIEWS)
        ]
    )
    own_tile = canvas[:, :, :rows, :cols]
    from_above = shifted(canvas[:, :, rows:, :cols], "gy", 1)
    from_left = shifted(canvas[:, :, :rows, cols:], "gx", 1)
    from_diagonal = shifted(canvas[:, :, rows:, cols:], ("gy", "gx"), lax.axis_size("gx") + 1)
    from_diagonal = from_diagonal * (lax.axis_index("gx") > 0).astype(jnp.float32)
    own_tile = own_tile.at[:, :, :REACH, :].add(from_above)
    own_tile = own_tile.at[:, :, :, :REACH].add(from_left)
    own_tile = own_tile.at[:, :, :REACH, :REACH].add(from_diagonal)
    ranking = precedence(order)
    pieces = lax.all_to_all(own_tile[None], "gz", split_axis=3, concat_axis=0, tiled=True)
    depths = pieces[:, :, 3]
    cover = jnp.einsum("vbc,cvyx->bvyx", ranking, depths, precision=lax.Precision.HIGHEST)
    colors = jnp.sum(pieces[:, :, :3] * jnp.exp(-cover)[:, :, None], axis=0)
    opacity = 1.0 - jnp.exp(-jnp.sum(depths, axis=0))
    image = jnp.concatenate([colors, opacity[:, None]], axis=1)
    return image[:, :, None]


def exchange(dims, mine, here, p_ref, m_ref, l_ref, r_ref, lpk, rpk, sends, arrivals, local_sem):
    ny, nx, bz, rows = dims
    z, y, x = here
    strip = rows // 2
    tall = HALO + strip + SUB
    per = LANES // HALO
    groups = -(-bz // per)
    other = 1 - mine
    first_lane = LANES - HALO
    has_up, has_down = y > 0, y < ny - 1
    has_left, has_right = x > 0, x < nx - 1

    def remote(src, dst, slot, arrival, who):
        return pltpu.make_async_remote_copy(
            src_ref=src,
            dst_ref=dst,
            send_sem=sends.at[slot],
            recv_sem=arrivals.at[arrival],
            device_id=who,
            device_id_type=MESH,
        )

    def spans(to):
        if to == 0:
            return pl.ds(0, strip + SUB), pl.ds(HALO, strip + SUB)
        return pl.ds(strip - HALO, HALO + strip), pl.ds(0, HALO + strip)

    def main(brick, g):
        count = min(per, bz - g * per)
        source, target = spans(1 - brick)
        return remote(
            p_ref.at[pl.ds(g * per, count), source],
            m_ref.at[pl.ds(1 + brick * bz + g * per, count), target],
            g, g, (1 - z, y, x),
        )

    def down(brick):
        return remote(
            p_ref.at[:, pl.ds(rows - HALO, HALO)],
            m_ref.at[pl.ds(1 + brick * bz, bz), pl.ds(0, HALO)],
            groups, groups + brick, (0, y + 1, x),
        )

    def up(brick):
        return remote(
            p_ref.at[:, pl.ds(0, SUB)],
            m_ref.at[pl.ds(1 + brick * bz, bz), pl.ds(HALO + strip, SUB)],
            groups + 1, groups + brick, (1, y - 1, x),
        )

    def rightward(brick, g):
        slot = groups + 2 + brick * groups + g
        return remote(
            lpk.at[brick * groups + g], l_ref.at[brick * groups + g], slot, slot, (z, y, x + 1)
        )

    def leftward(brick):
        slot = 3 * groups + 2 + brick
        return remote(rpk.at[brick], r_ref.at[brick], slot, slot, (z, y, x - 1))

    def started(there, copy):
        @pl.when(there)
        def _():
            copy.start()

    def arrived(there, copy):
        @pl.when(there)
        def _():
            copy.wait_recv()

    def left(there, copy):
        @pl.when(there)
        def _():
            copy.wait_send()

    lane = lax.broadcasted_iota(jnp.int32, (tall, LANES), 1)

    def pack(brick, g):
        packed = jnp.zeros((tall, LANES), jnp.float32)
        for j in range(min(per, bz - g * per)):
            cells = m_ref[1 + brick * bz + g * per + j]
            moved = pltpu.roll(cells, (j * HALO - first_lane) % LANES, 1)
            packed = jnp.where(lane >= j * HALO, moved, packed)
        lpk[brick * groups + g] = packed

    def pack_ends(brick):
        ends = jnp.zeros((tall, LANES), jnp.float32)
        for j in range(bz):
            cells = m_ref[1 + brick * bz + j]
            ends = jnp.where(lane == j, pltpu.roll(cells, j, 1) if j else cells, ends)
        rpk[brick] = ends

    def halo_in(brick):
        if mine == 0:
            arrived(has_up, down(brick))
        else:
            arrived(has_down, up(brick))

    def open_up():
        source, target = spans(mine)
        own = pltpu.make_async_copy(
            p_ref.at[:, source], m_ref.at[pl.ds(1 + mine * bz, bz), target], local_sem
        )
        started(has_down, down(mine))
        started(has_up, up(mine))
        for g in range(groups):
            main(mine, g).start()
        own.start()
        own.wait()
        halo_in(mine)
        for g in range(groups):
            pack(mine, g)
            started(has_right, rightward(mine, g))
        pack_ends(mine)
        started(has_left, leftward(mine))
        halo_in(other)
        for g in range(groups):
            main(other, g).wait_recv()
            pack(other, g)
            started(has_right, rightward(other, g))
        pack_ends(other)
        started(has_left, leftward(other))

    def columns_in(brick):
        for g in range(groups):
            arrived(has_left, rightward(brick, g))
        arrived(has_right, leftward(brick))

    def close():
        for g in range(groups):
            main(mine, g).wait_send()
        left(has_down, down(mine))
        left(has_up, up(mine))
        for brick in range(2):
            for g in range(groups):
                left(has_right, rightward(brick, g))
            left(has_left, leftward(brick))

    return open_up, columns_in, close


def render(
    dims, light, palette, rate, shear, offset, order, p_ref, out_ref,
    m_ref, l_ref, r_ref, lpk, rpk, h_ref, dm, dh, sends, arrivals, local_sem,
):
    ny, nx, bz, rows = dims
    strip = rows // 2
    tall = HALO + strip + SUB
    depth = 2 * bz
    per = LANES // HALO
    groups = -(-bz // per)
    first_lane = LANES - HALO
    z, y, x = lax.axis_index("gz"), lax.axis_index("gy"), lax.axis_index("gx")
    has_up, has_down = y > 0, y < ny - 1
    has_left, has_right = x > 0, x < nx - 1

    empty = jnp.zeros((tall, LANES), jnp.float32)
    for ref in (m_ref, h_ref):
        ref[0] = empty
        ref[depth + 1] = empty

    @pl.when(jnp.logical_and(z == 0, y == 0))
    def _():
        m_ref[:, :HALO] = jnp.zeros((depth + 2, HALO, LANES), jnp.float32)

    @pl.when(jnp.logical_and(z == 1, y == ny - 1))
    def _():
        m_ref[:, HALO + strip :] = jnp.zeros((depth + 2, SUB, LANES), jnp.float32)

    @pl.when(x == 0)
    def _():
        l_ref[...] = jnp.zeros(l_ref.shape, jnp.float32)

    @pl.when(x == nx - 1)
    def _():
        r_ref[...] = jnp.zeros(r_ref.shape, jnp.float32)

    cross = y + 2 * z - 1
    partners = (
        (y >= 0, (1 - z, y, x)),
        (has_up, (z, y - 1, x)),
        (has_down, (z, y + 1, x)),
        (jnp.logical_and(cross >= 0, cross < ny), (1 - z, cross, x)),
        (has_left, (z, y, x - 1)),
        (has_right, (z, y, x + 1)),
    )
    barrier = pltpu.get_barrier_semaphore()
    count = 0
    for there, who in partners:

        @pl.when(there)
        def _():
            pl.semaphore_signal(barrier, inc=1, device_id=who, device_id_type=MESH)

        count = count + there.astype(jnp.int32)
    pl.semaphore_wait(barrier, count)

    steps = [
        exchange(
            dims, mine, (z, y, x), p_ref, m_ref, l_ref, r_ref, lpk, rpk, sends, arrivals, local_sem
        )
        for mine in range(2)
    ]

    for mine in range(2):

        @pl.when(z == mine)
        def _():
            steps[mine][0]()
            steps[mine][1](mine)

    def unpack(brick):
        for j in range(bz):
            shift = (first_lane - (j % per) * HALO) % LANES
            h_ref[1 + brick * bz + j] = pltpu.roll(l_ref[brick * groups + j // per], shift, 1)

    towards = []
    for w in range(VIEWS):
        a, b, c = light[w, 0], light[w, 1], light[w, 2]
        inverse = lax.rsqrt(jnp.full((SUB, LANES), a * a + b * b + c * c + 1.0, jnp.float32))
        towards.append((a * inverse, b * inverse, c * inverse))

    lane = lax.broadcasted_iota(jnp.int32, (SUB, LANES), 1)
    last = lane == LANES - 1
    first = lane == 0

    def slopes(k, carry):
        for i in range((HALO + strip) // SUB):
            top = i * SUB
            here = m_ref[k + 1, top + 1 : top + 1 + SUB]
            side = h_ref[k + 1, top + 1 : top + 1 + SUB]
            beyond = pltpu.roll(r_ref[k // bz, top + 1 : top + 1 + SUB], LANES - 1 - k % bz, 1)
            here_r, here_l = pltpu.roll(here, LANES - 1, 1), pltpu.roll(here, 1, 1)
            side_r, side_l = pltpu.roll(side, LANES - 1, 1), pltpu.roll(side, 1, 1)
            for ref, cols, dots in (
                (m_ref, jnp.where(last, beyond, here_r) - jnp.where(first, side_l, here_l), dm),
                (h_ref, jnp.where(last, here_r, side_r) - side_l, dh),
            ):
                deep = ref[k + 2, top + 1 : top + 1 + SUB] - ref[k, top + 1 : top + 1 + SUB]
                down = ref[k + 1, top + 2 : top + 2 + SUB] - ref[k + 1, top : top + SUB]
                half = 0.5 * lax.rsqrt(0.25 * (deep * deep + down * down + cols * cols) + 1.0)
                deep, down, cols = deep * half, down * half, cols * half
                for w in range(VIEWS):
                    a, b, c = towards[w]
                    dots[w, k, top : top + SUB] = deep * a + down * b + cols * c
        return carry

    unpack(z)
    lax.fori_loop(z * (bz + 1), z * (bz + 1) + bz - 1, slopes, 0)

    for mine in range(2):

        @pl.when(z == mine)
        def _():
            steps[mine][1](1 - mine)
            steps[mine][2]()

    unpack(1 - z)
    lax.fori_loop((1 - z) * (bz - 1), (1 - z) * (bz - 1) + bz + 1, slopes, 0)

    tile = 32
    base_row = y * rows + z * strip
    base_col = x * LANES
    lanes = lax.broadcasted_iota(jnp.int32, (tile, LANES), 1)
    rows_at = lax.broadcasted_iota(jnp.int32, (tile, LANES), 0)
    bias = [0.5 * palette[0, c] for c in range(3)]
    gain = [0.5 * palette[1, c] for c in range(3)]

    def view_part(step, carry):
        w = step // (strip // tile)
        top = (step % (strip // tile)) * tile
        through = jnp.ones((tile, LANES), jnp.float32)
        ambient = jnp.zeros((tile, LANES), jnp.float32)
        colors = [jnp.zeros((tile, LANES), jnp.float32) for _ in range(3)]
        rate2 = rate[w] * (-math.log2(math.e))
        for place in range(2):
            brick = order[place, w]
            off_r, off_c = offset[brick, 0, w], offset[brick, 1, w]
            inside = jnp.logical_and(
                rows_at >= off_r - base_row - top, lanes >= off_c - base_col
            )
            fall = jnp.where(inside, rate2, 0.0)
            for j in range(bz):
                k = brick * bz + j
                sr = off_r + shear[w, 0, k]
                sc = off_c + shear[w, 1, k]
                at = HALO + top - sr
                wrap = lanes >= LANES - sc
                value = jnp.where(
                    wrap, h_ref[k + 1, pl.ds(at, tile)], m_ref[k + 1, pl.ds(at, tile)]
                )
                dot = jnp.where(wrap, dh[w, k, pl.ds(at - 1, tile)], dm[w, k, pl.ds(at - 1, tile)])
                value = pltpu.roll(value, sc, 1)
                dot = pltpu.roll(dot, sc, 1)
                kept = jnp.exp2(fall * (1.0 + jnp.tanh(value)))
                weight = (0.125 + 0.375 * dot * dot) * ((1.0 - kept) * through)
                through = through * kept
                ambient = ambient + weight
                for c in range(3):
                    colors[c] = colors[c] + weight * jnp.tanh(bias[c] + gain[c] * value)
        for c in range(3):
            out_ref[w, c, pl.ds(top, tile)] = ambient + colors[c]
        out_ref[w, 3, pl.ds(top, tile)] = 1.0 - through
        return carry

    lax.fori_loop(0, VIEWS * (strip // tile), view_part, 0)


def two_bricks(mesh, pressure, light, palette, rate, shear, offset, order):
    bz, rows, cols = pressure.shape
    dims = (mesh.shape["gy"], mesh.shape["gx"], bz, rows)
    strip = rows // 2
    tall = HALO + strip + SUB
    depth = 2 * bz
    groups = -(-bz // (LANES // HALO))
    vmem = pl.BlockSpec(memory_space=pltpu.VMEM)
    smem = pl.BlockSpec(memory_space=pltpu.SMEM)
    f32 = jnp.float32
    copies = 3 * groups + 4
    image = pl.pallas_call(
        functools.partial(render, dims),
        out_shape=jax.ShapeDtypeStruct((VIEWS, 4, strip, LANES), f32),
        in_specs=[smem] * 6 + [pl.BlockSpec(memory_space=pl.ANY)],
        out_specs=vmem,
        scratch_shapes=[
            pltpu.VMEM((depth + 2, tall, LANES), f32),
            pltpu.VMEM((2 * groups, tall, LANES), f32),
            pltpu.VMEM((2, tall, LANES), f32),
            pltpu.VMEM((2 * groups, tall, LANES), f32),
            pltpu.VMEM((2, tall, LANES), f32),
            pltpu.VMEM((depth + 2, tall, LANES), f32),
            pltpu.VMEM((VIEWS, depth, HALO + strip, LANES), f32),
            pltpu.VMEM((VIEWS, depth, HALO + strip, LANES), f32),
            pltpu.SemaphoreType.DMA((copies,)),
            pltpu.SemaphoreType.DMA((copies,)),
            pltpu.SemaphoreType.DMA,
        ],
        compiler_params=pltpu.CompilerParams(collective_id=0, has_side_effects=True),
        name="render",
    )(
        light,
        palette.T,
        rate,
        jnp.transpose(shear, (0, 2, 1)),
        jnp.transpose(offset, (1, 2, 0)),
        order.T,
        pressure,
    )
    return image[:, :, None]


def on_device(mesh, pressure, *rest):
    bz, rows, cols = pressure.shape
    if mesh.shape["gz"] == 2 and cols == LANES and rows % 64 == 0 and rows // 2 >= HALO:
        return two_bricks(mesh, pressure, *rest)
    return many_bricks(pressure, *rest)


def solution(mesh):
    return jax.shard_map(
        functools.partial(on_device, mesh),
        mesh=mesh,
        in_specs=(P("gz", "gy", "gx"), P(), P(), P(), P(), P(), P()),
        out_specs=P(None, None, "gz", "gy", "gx"),
        check_vma=False,
    )
```

```python
import functools
import math

import jax
import jax.numpy as jnp
from jax import lax
from jax.experimental import pallas as pl
from jax.experimental.pallas import tpu as pltpu
from jax.sharding import PartitionSpec as P

VIEWS = 4
SHEAR = 8
REACH = 32
HALO = SHEAR + REACH
SUB = 8
BLOCK = 16
LANES = 128
MESH = pl.DeviceIdType.MESH


def padded(cells, sides, width):
    for axis, dim in sides:
        count = lax.axis_size(axis)
        ends = count - 1
        head = lax.slice_in_dim(cells, 0, width, axis=dim)
        tail = lax.slice_in_dim(cells, cells.shape[dim] - width, cells.shape[dim], axis=dim)
        cells = jnp.concatenate(
            [
                lax.ppermute(tail, axis, [(i, (i + 1) % count) for i in range(ends)]),
                cells,
                lax.ppermute(head, axis, [((i + 1) % count, i) for i in range(ends)]),
            ],
            axis=dim,
        )
    return cells


def shifted(value, axis, steps):
    count = lax.axis_size(axis)
    first, last = (max(0, -steps), min(count, count - steps))
    return lax.ppermute(value, axis, [(source, source + steps) for source in range(first, last)])


def surface_terms(slab):
    inner = slab[1:-1, 1:-1, 1:-1]
    grad_depth = 0.5 * (slab[2:, 1:-1, 1:-1] - slab[:-2, 1:-1, 1:-1])
    grad_rows = 0.5 * (slab[1:-1, 2:, 1:-1] - slab[1:-1, :-2, 1:-1])
    grad_cols = 0.5 * (slab[1:-1, 1:-1, 2:] - slab[1:-1, 1:-1, :-2])
    factor = lax.rsqrt(
        grad_depth * grad_depth + grad_rows * grad_rows + grad_cols * grad_cols + 1.0
    )
    return (inner, (grad_depth * factor, grad_rows * factor, grad_cols * factor))


def render_layers(inner, normals, shifts, light, palette, rate, rows, cols):
    lengths = jnp.sqrt(jnp.sum(light * light, axis=1, keepdims=True) + 1.0)
    towards = light / lengths
    offsets = palette[:, 0][:, None, None]
    slopes = palette[:, 1][:, None, None]
    layers = []
    for view in range(light.shape[0]):

        def advance(carry, items):
            color, depth = carry
            value_slab, normal_depth, normal_rows, normal_cols, moved = items
            start = (SHEAR - moved[0], SHEAR - moved[1])
            value = lax.dynamic_slice(value_slab, start, (rows, cols))
            dot = (
                lax.dynamic_slice(normal_depth, start, (rows, cols)) * towards[view, 0]
                + lax.dynamic_slice(normal_rows, start, (rows, cols)) * towards[view, 1]
                + lax.dynamic_slice(normal_cols, start, (rows, cols)) * towards[view, 2]
            )
            shade = 0.25 + 0.75 * dot * dot
            density = rate[view] * (1.0 + jnp.tanh(value))
            alpha = 1.0 - jnp.exp(-density)
            weight = alpha * jnp.exp(-depth)
            hues = jax.nn.sigmoid(offsets + slopes * value[None]) * shade[None]
            return ((color + hues * weight[None], depth + density), None)

        start_carry = (
            jnp.zeros((3, rows, cols), jnp.float32),
            jnp.zeros((rows, cols), jnp.float32),
        )
        (color, depth), _ = lax.scan(
            advance, start_carry, (inner, normals[0], normals[1], normals[2], shifts[view])
        )
        layers.append(jnp.concatenate([color, depth[None]], axis=0))
    return jnp.stack(layers)


def precedence(order):
    bricks = order.shape[1]
    onehot = (order[:, :, None] == jnp.arange(bricks, dtype=jnp.int32)[None, None, :]).astype(
        jnp.float32
    )
    ranks = jnp.sum(onehot * jnp.arange(bricks, dtype=jnp.float32)[None, :, None], axis=1)
    return (ranks[:, None, :] < ranks[:, :, None]).astype(jnp.float32)


def many_bricks(pressure, light, palette, rate, shear, offset, order):
    depth_cells, rows, cols = pressure.shape
    brick = lax.axis_index("gz")
    zero = jnp.zeros((), jnp.int32)
    widened = padded(pressure, (("gy", 1), ("gx", 2)), SHEAR + 1)
    slab = padded(widened, (("gz", 0),), 1)
    inner, normals = surface_terms(slab)
    shifts = lax.dynamic_slice(shear, (zero, brick * depth_cells, zero), (VIEWS, depth_cells, 2))
    layers = render_layers(inner, normals, shifts, light, palette, rate, rows, cols)
    moved = lax.dynamic_index_in_dim(offset, brick, 1, keepdims=False)
    blank = jnp.zeros((4, rows + REACH, cols + REACH), jnp.float32)
    canvas = jnp.stack(
        [
            lax.dynamic_update_slice(blank, layers[view], (zero, moved[view, 0], moved[view, 1]))
            for view in range(VIEWS)
        ]
    )
    own_tile = canvas[:, :, :rows, :cols]
    from_above = shifted(canvas[:, :, rows:, :cols], "gy", 1)
    from_left = shifted(canvas[:, :, :rows, cols:], "gx", 1)
    from_diagonal = shifted(canvas[:, :, rows:, cols:], ("gy", "gx"), lax.axis_size("gx") + 1)
    from_diagonal = from_diagonal * (lax.axis_index("gx") > 0).astype(jnp.float32)
    own_tile = own_tile.at[:, :, :REACH, :].add(from_above)
    own_tile = own_tile.at[:, :, :, :REACH].add(from_left)
    own_tile = own_tile.at[:, :, :REACH, :REACH].add(from_diagonal)
    ranking = precedence(order)
    pieces = lax.all_to_all(own_tile[None], "gz", split_axis=3, concat_axis=0, tiled=True)
    depths = pieces[:, :, 3]
    cover = jnp.einsum("vbc,cvyx->bvyx", ranking, depths, precision=lax.Precision.HIGHEST)
    colors = jnp.sum(pieces[:, :, :3] * jnp.exp(-cover)[:, :, None], axis=0)
    opacity = 1.0 - jnp.exp(-jnp.sum(depths, axis=0))
    image = jnp.concatenate([colors, opacity[:, None]], axis=1)
    return image[:, :, None]


def segments(tall):
    return (0, HALO, tall - HALO)


def exchange(
    dims, mine, here, p_ref, m_ref, full_in, rest_in, ends_in, full_out, rest_out, ends_out, sends,
    arrivals, local_sem,
):
    ny, nx, bz, rows = dims
    z, y, x = here
    strip = rows // 2
    tall = HALO + strip + SUB
    per = LANES // HALO
    groups = -(-bz // per)
    other = 1 - mine
    first_lane = LANES - HALO
    has_up, has_down = y > 0, y < ny - 1
    has_left, has_right = x > 0, x < nx - 1

    def remote(src, dst, slot, arrival, who):
        return pltpu.make_async_remote_copy(
            src_ref=src,
            dst_ref=dst,
            send_sem=sends.at[slot],
            recv_sem=arrivals.at[arrival],
            device_id=who,
            device_id_type=MESH,
        )

    def spans(to):
        if to == 0:
            return pl.ds(0, strip + SUB), pl.ds(HALO, strip + SUB)
        return pl.ds(strip - HALO, HALO + strip), pl.ds(0, HALO + strip)

    def main(brick, g):
        count = min(per, bz - g * per)
        source, target = spans(1 - brick)
        return remote(
            p_ref.at[pl.ds(g * per, count), source],
            m_ref.at[pl.ds(1 + brick * bz + g * per, count), target],
            g, g, (1 - z, y, x),
        )

    def down(brick):
        return remote(
            p_ref.at[:, pl.ds(rows - HALO, HALO)],
            m_ref.at[pl.ds(1 + brick * bz, bz), pl.ds(0, HALO)],
            groups, groups + brick, (0, y + 1, x),
        )

    def up(brick):
        return remote(
            p_ref.at[:, pl.ds(0, SUB)],
            m_ref.at[pl.ds(1 + brick * bz, bz), pl.ds(HALO + strip, SUB)],
            groups + 1, groups + brick, (1, y - 1, x),
        )

    def rightward(brick, g):
        slot = groups + 2 + brick * groups + g
        if g == groups - 1:
            return remote(rest_out.at[brick], rest_in.at[brick], slot, slot, (z, y, x + 1))
        at = brick * (groups - 1) + g
        return remote(full_out.at[at], full_in.at[at], slot, slot, (z, y, x + 1))

    def leftward(brick):
        slot = 3 * groups + 2 + brick
        return remote(ends_out.at[brick], ends_in.at[brick], slot, slot, (z, y, x - 1))

    def started(there, copy):
        @pl.when(there)
        def _():
            copy.start()

    def arrived(there, copy):
        @pl.when(there)
        def _():
            copy.wait_recv()

    def left(there, copy):
        @pl.when(there)
        def _():
            copy.wait_send()

    def pack(brick, g):
        if g == groups - 1:
            lane = lax.broadcasted_iota(jnp.int32, (HALO, LANES), 1)
            pieces = [m_ref[brick * bz + bz, row : row + HALO] for row in segments(tall)]
        else:
            lane = lax.broadcasted_iota(jnp.int32, (tall, LANES), 1)
            pieces = [m_ref[1 + brick * bz + g * per + j] for j in range(per)]
        packed = pltpu.roll(pieces[0], LANES - first_lane, 1)
        for j in range(1, per):
            moved = pltpu.roll(pieces[j], (j * HALO - first_lane) % LANES, 1)
            packed = jnp.where(lane >= j * HALO, moved, packed)
        if g == groups - 1:
            rest_out[brick] = packed
        else:
            full_out[brick * (groups - 1) + g] = packed

    def pack_ends(brick):
        lane = lax.broadcasted_iota(jnp.int32, (BLOCK, LANES), 1)
        ends = jnp.zeros((BLOCK, LANES), jnp.float32)
        for j in range(bz):
            for i in range(tall // BLOCK):
                at = i * bz + j
                cells = m_ref[1 + brick * bz + j, i * BLOCK : (i + 1) * BLOCK]
                ends = jnp.where(lane == at, pltpu.roll(cells, at, 1) if at else cells, ends)
        ends_out[brick] = ends

    def halo_in(brick):
        if mine == 0:
            arrived(has_up, down(brick))
        else:
            arrived(has_down, up(brick))

    def open_up():
        source, target = spans(mine)
        own = pltpu.make_async_copy(
            p_ref.at[:, source], m_ref.at[pl.ds(1 + mine * bz, bz), target], local_sem
        )
        started(has_down, down(mine))
        started(has_up, up(mine))
        for g in range(groups):
            main(mine, g).start()
        own.start()
        own.wait()
        halo_in(mine)
        for g in range(groups):
            pack(mine, g)
            started(has_right, rightward(mine, g))
        pack_ends(mine)
        started(has_left, leftward(mine))
        halo_in(other)
        for g in range(groups):
            main(other, g).wait_recv()
            pack(other, g)
            started(has_right, rightward(other, g))
        pack_ends(other)
        started(has_left, leftward(other))

    def columns_in(brick):
        for g in range(groups):
            arrived(has_left, rightward(brick, g))
        arrived(has_right, leftward(brick))

    def close():
        for g in range(groups):
            main(mine, g).wait_send()
        left(has_down, down(mine))
        left(has_up, up(mine))
        for brick in range(2):
            for g in range(groups):
                left(has_right, rightward(brick, g))
            left(has_left, leftward(brick))

    return open_up, columns_in, close


def render(
    dims, light_in, palette_in, rate_in, shear_in, offset_in, order_in, p_ref, out_ref,
    light, palette, rate, shear, offset, order, m_ref, full_in, rest_in, ends_in,
    full_out, rest_out, ends_out, h_ref, r_ref, dm, dh, sends, arrivals, local_sem, table_sems,
):
    ny, nx, bz, rows = dims
    strip = rows // 2
    tall = HALO + strip + SUB
    depth = 2 * bz
    per = LANES // HALO
    groups = -(-bz // per)
    first_lane = LANES - HALO
    z, y, x = lax.axis_index("gz"), lax.axis_index("gy"), lax.axis_index("gx")
    has_up, has_down = y > 0, y < ny - 1
    has_left, has_right = x > 0, x < nx - 1

    tables = [
        pltpu.make_async_copy(source, target, table_sems.at[i])
        for i, (source, target) in enumerate(
            (
                (light_in, light), (palette_in, palette), (rate_in, rate),
                (shear_in, shear), (offset_in, offset), (order_in, order),
            )
        )
    ]
    for copy in tables:
        copy.start()

    empty = jnp.zeros((tall, LANES), jnp.float32)
    for ref in (m_ref, h_ref):
        ref[0] = empty
        ref[depth + 1] = empty

    @pl.when(jnp.logical_and(z == 0, y == 0))
    def _():
        m_ref[:, :HALO] = jnp.zeros((depth + 2, HALO, LANES), jnp.float32)

    @pl.when(jnp.logical_and(z == 1, y == ny - 1))
    def _():
        m_ref[:, HALO + strip :] = jnp.zeros((depth + 2, SUB, LANES), jnp.float32)

    @pl.when(x == 0)
    def _():
        full_in[...] = jnp.zeros(full_in.shape, jnp.float32)
        rest_in[...] = jnp.zeros(rest_in.shape, jnp.float32)

    @pl.when(x == nx - 1)
    def _():
        ends_in[...] = jnp.zeros(ends_in.shape, jnp.float32)

    cross = y + 2 * z - 1
    partners = (
        (y >= 0, (1 - z, y, x)),
        (has_up, (z, y - 1, x)),
        (has_down, (z, y + 1, x)),
        (jnp.logical_and(cross >= 0, cross < ny), (1 - z, cross, x)),
        (has_left, (z, y, x - 1)),
        (has_right, (z, y, x + 1)),
    )
    barrier = pltpu.get_barrier_semaphore()
    count = 0
    for there, who in partners:

        @pl.when(there)
        def _():
            pl.semaphore_signal(barrier, inc=1, device_id=who, device_id_type=MESH)

        count = count + there.astype(jnp.int32)
    pl.semaphore_wait(barrier, count)

    steps = [
        exchange(
            dims, mine, (z, y, x), p_ref, m_ref, full_in, rest_in, ends_in, full_out, rest_out,
            ends_out, sends, arrivals, local_sem,
        )
        for mine in range(2)
    ]

    for mine in range(2):

        @pl.when(z == mine)
        def _():
            steps[mine][0]()
            steps[mine][1](mine)

    def unpack(brick):
        for j in range(bz - 1):
            shift = (first_lane - (j % per) * HALO) % LANES
            cells = full_in[brick * (groups - 1) + j // per]
            h_ref[1 + brick * bz + j] = pltpu.roll(cells, shift, 1)
        cells = rest_in[brick]
        for j, row in enumerate(segments(tall)):
            moved = pltpu.roll(cells, (first_lane - j * HALO) % LANES, 1)
            h_ref[brick * bz + bz, row : row + HALO] = moved
        cells = ends_in[brick]
        for i in range(tall // BLOCK):
            moved = pltpu.roll(cells, (LANES - 1 - i * bz) % LANES, 1)
            r_ref[brick, i * BLOCK : (i + 1) * BLOCK] = moved

    for copy in tables:
        copy.wait()

    towards = []
    for w in range(VIEWS):
        a, b, c = light[w, 0], light[w, 1], light[w, 2]
        inverse = lax.rsqrt(jnp.full((SUB, LANES), a * a + b * b + c * c + 1.0, jnp.float32))
        towards.append((a * inverse, b * inverse, c * inverse))

    lane = lax.broadcasted_iota(jnp.int32, (SUB, LANES), 1)
    last = lane == LANES - 1
    first = lane == 0

    def slopes(k, carry):
        for i in range((HALO + strip) // SUB):
            top = i * SUB
            here = m_ref[k + 1, top + 1 : top + 1 + SUB]
            side = h_ref[k + 1, top + 1 : top + 1 + SUB]
            beyond = pltpu.roll(
                r_ref[k // bz, top + 1 : top + 1 + SUB], (LANES - k % bz) % LANES, 1
            )
            here_r, here_l = pltpu.roll(here, LANES - 1, 1), pltpu.roll(here, 1, 1)
            side_r, side_l = pltpu.roll(side, LANES - 1, 1), pltpu.roll(side, 1, 1)
            for ref, cols, dots in (
                (m_ref, jnp.where(last, beyond, here_r) - jnp.where(first, side_l, here_l), dm),
                (h_ref, jnp.where(last, here_r, side_r) - side_l, dh),
            ):
                deep = ref[k + 2, top + 1 : top + 1 + SUB] - ref[k, top + 1 : top + 1 + SUB]
                down = ref[k + 1, top + 2 : top + 2 + SUB] - ref[k + 1, top : top + SUB]
                half = 0.5 * lax.rsqrt(0.25 * (deep * deep + down * down + cols * cols) + 1.0)
                deep, down, cols = deep * half, down * half, cols * half
                for w in range(VIEWS):
                    a, b, c = towards[w]
                    dots[w, k, top : top + SUB] = deep * a + down * b + cols * c
        return carry

    unpack(z)
    lax.fori_loop(z * (bz + 1), z * (bz + 1) + bz - 1, slopes, 0)

    for mine in range(2):

        @pl.when(z == mine)
        def _():
            steps[mine][1](1 - mine)
            steps[mine][2]()

    unpack(1 - z)
    lax.fori_loop((1 - z) * (bz - 1), (1 - z) * (bz - 1) + bz + 1, slopes, 0)

    tile = 32
    base_row = y * rows + z * strip
    base_col = x * LANES
    lanes = lax.broadcasted_iota(jnp.int32, (tile, LANES), 1)
    rows_at = lax.broadcasted_iota(jnp.int32, (tile, LANES), 0)
    bias = [0.5 * palette[0, c] for c in range(3)]
    gain = [0.5 * palette[1, c] for c in range(3)]

    def view_part(step, carry):
        w = step // (strip // tile)
        top = (step % (strip // tile)) * tile
        through = jnp.ones((tile, LANES), jnp.float32)
        ambient = jnp.zeros((tile, LANES), jnp.float32)
        colors = [jnp.zeros((tile, LANES), jnp.float32) for _ in range(3)]
        rate2 = rate[w] * (-math.log2(math.e))
        for place in range(2):
            brick = order[place, w]
            off_r, off_c = offset[brick, 0, w], offset[brick, 1, w]
            inside = jnp.logical_and(
                rows_at >= off_r - base_row - top, lanes >= off_c - base_col
            )
            fall = jnp.where(inside, rate2, 0.0)
            for j in range(bz):
                k = brick * bz + j
                sr = off_r + shear[w, 0, k]
                sc = off_c + shear[w, 1, k]
                at = HALO + top - sr
                wrap = lanes >= LANES - sc
                value = jnp.where(
                    wrap, h_ref[k + 1, pl.ds(at, tile)], m_ref[k + 1, pl.ds(at, tile)]
                )
                dot = jnp.where(wrap, dh[w, k, pl.ds(at - 1, tile)], dm[w, k, pl.ds(at - 1, tile)])
                value = pltpu.roll(value, sc, 1)
                dot = pltpu.roll(dot, sc, 1)
                kept = jnp.exp2(fall * (1.0 + jnp.tanh(value)))
                weight = (0.125 + 0.375 * dot * dot) * ((1.0 - kept) * through)
                through = through * kept
                ambient = ambient + weight
                for c in range(3):
                    colors[c] = colors[c] + weight * jnp.tanh(bias[c] + gain[c] * value)
        for c in range(3):
            out_ref[w, c, pl.ds(top, tile)] = ambient + colors[c]
        out_ref[w, 3, pl.ds(top, tile)] = 1.0 - through
        return carry

    lax.fori_loop(0, VIEWS * (strip // tile), view_part, 0)


def two_bricks(mesh, pressure, light, palette, rate, shear, offset, order):
    bz, rows, cols = pressure.shape
    dims = (mesh.shape["gy"], mesh.shape["gx"], bz, rows)
    strip = rows // 2
    tall = HALO + strip + SUB
    depth = 2 * bz
    groups = -(-bz // (LANES // HALO))
    vmem = pl.BlockSpec(memory_space=pltpu.VMEM)
    hbm = pl.BlockSpec(memory_space=pltpu.HBM)
    f32 = jnp.float32
    copies = 3 * groups + 4
    tables = (
        light,
        palette.T,
        rate,
        jnp.transpose(shear, (0, 2, 1)),
        jnp.transpose(offset, (1, 2, 0)),
        order.T,
    )
    image = pl.pallas_call(
        functools.partial(render, dims),
        out_shape=jax.ShapeDtypeStruct((VIEWS, 4, strip, LANES), f32),
        in_specs=[hbm] * 7,
        out_specs=vmem,
        scratch_shapes=[
            *[pltpu.SMEM(table.shape, table.dtype) for table in tables],
            pltpu.VMEM((depth + 2, tall, LANES), f32),
            pltpu.VMEM((2 * groups - 2, tall, LANES), f32),
            pltpu.VMEM((2, HALO, LANES), f32),
            pltpu.VMEM((2, BLOCK, LANES), f32),
            pltpu.VMEM((2 * groups - 2, tall, LANES), f32),
            pltpu.VMEM((2, HALO, LANES), f32),
            pltpu.VMEM((2, BLOCK, LANES), f32),
            pltpu.VMEM((depth + 2, tall, LANES), f32),
            pltpu.VMEM((2, tall, LANES), f32),
            pltpu.VMEM((VIEWS, depth, HALO + strip, LANES), f32),
            pltpu.VMEM((VIEWS, depth, HALO + strip, LANES), f32),
            pltpu.SemaphoreType.DMA((copies,)),
            pltpu.SemaphoreType.DMA((copies,)),
            pltpu.SemaphoreType.DMA,
            pltpu.SemaphoreType.DMA((len(tables),)),
        ],
        compiler_params=pltpu.CompilerParams(collective_id=0, has_side_effects=True, vmem_limit_bytes=12 << 20),
        name="render",
    )(
        *[pltpu.with_memory_space_constraint(t, pltpu.HBM) for t in (*tables, pressure)]
    )
    return image[:, :, None]


def fits(mesh, shape):
    bz, rows, cols = shape
    tall = HALO + rows // 2 + SUB
    return (
        mesh.shape["gz"] == 2
        and cols == LANES
        and rows % 64 == 0
        and 2 * HALO <= tall <= 3 * HALO
        and tall % BLOCK == 0
        and bz % (LANES // HALO) == 1
        and bz * (tall // BLOCK) <= LANES
    )


def on_device(mesh, pressure, *rest):
    if fits(mesh, pressure.shape):
        return two_bricks(mesh, pressure, *rest)
    return many_bricks(pressure, *rest)


def solution(mesh):
    return jax.shard_map(
        functools.partial(on_device, mesh),
        mesh=mesh,
        in_specs=(P("gz", "gy", "gx"), P(), P(), P(), P(), P(), P()),
        out_specs=P(None, None, "gz", "gy", "gx"),
        check_vma=False,
    )
```

```python
import functools
import math

import jax
import jax.numpy as jnp
from jax import lax
from jax.experimental import pallas as pl
from jax.experimental.pallas import tpu as pltpu
from jax.sharding import PartitionSpec as P

VIEWS = 4
SHEAR = 8
REACH = 32
HALO = SHEAR + REACH
SUB = 8
BLOCK = 16
LANES = 128
MESH = pl.DeviceIdType.MESH


def padded(cells, sides, width):
    for axis, dim in sides:
        count = lax.axis_size(axis)
        ends = count - 1
        head = lax.slice_in_dim(cells, 0, width, axis=dim)
        tail = lax.slice_in_dim(cells, cells.shape[dim] - width, cells.shape[dim], axis=dim)
        cells = jnp.concatenate(
            [
                lax.ppermute(tail, axis, [(i, (i + 1) % count) for i in range(ends)]),
                cells,
                lax.ppermute(head, axis, [((i + 1) % count, i) for i in range(ends)]),
            ],
            axis=dim,
        )
    return cells


def shifted(value, axis, steps):
    count = lax.axis_size(axis)
    first, last = (max(0, -steps), min(count, count - steps))
    return lax.ppermute(value, axis, [(source, source + steps) for source in range(first, last)])


def surface_terms(slab):
    inner = slab[1:-1, 1:-1, 1:-1]
    grad_depth = 0.5 * (slab[2:, 1:-1, 1:-1] - slab[:-2, 1:-1, 1:-1])
    grad_rows = 0.5 * (slab[1:-1, 2:, 1:-1] - slab[1:-1, :-2, 1:-1])
    grad_cols = 0.5 * (slab[1:-1, 1:-1, 2:] - slab[1:-1, 1:-1, :-2])
    factor = lax.rsqrt(
        grad_depth * grad_depth + grad_rows * grad_rows + grad_cols * grad_cols + 1.0
    )
    return (inner, (grad_depth * factor, grad_rows * factor, grad_cols * factor))


def render_layers(inner, normals, shifts, light, palette, rate, rows, cols):
    lengths = jnp.sqrt(jnp.sum(light * light, axis=1, keepdims=True) + 1.0)
    towards = light / lengths
    offsets = palette[:, 0][:, None, None]
    slopes = palette[:, 1][:, None, None]
    layers = []
    for view in range(light.shape[0]):

        def advance(carry, items):
            color, depth = carry
            value_slab, normal_depth, normal_rows, normal_cols, moved = items
            start = (SHEAR - moved[0], SHEAR - moved[1])
            value = lax.dynamic_slice(value_slab, start, (rows, cols))
            dot = (
                lax.dynamic_slice(normal_depth, start, (rows, cols)) * towards[view, 0]
                + lax.dynamic_slice(normal_rows, start, (rows, cols)) * towards[view, 1]
                + lax.dynamic_slice(normal_cols, start, (rows, cols)) * towards[view, 2]
            )
            shade = 0.25 + 0.75 * dot * dot
            density = rate[view] * (1.0 + jnp.tanh(value))
            alpha = 1.0 - jnp.exp(-density)
            weight = alpha * jnp.exp(-depth)
            hues = jax.nn.sigmoid(offsets + slopes * value[None]) * shade[None]
            return ((color + hues * weight[None], depth + density), None)

        start_carry = (
            jnp.zeros((3, rows, cols), jnp.float32),
            jnp.zeros((rows, cols), jnp.float32),
        )
        (color, depth), _ = lax.scan(
            advance, start_carry, (inner, normals[0], normals[1], normals[2], shifts[view])
        )
        layers.append(jnp.concatenate([color, depth[None]], axis=0))
    return jnp.stack(layers)


def precedence(order):
    bricks = order.shape[1]
    onehot = (order[:, :, None] == jnp.arange(bricks, dtype=jnp.int32)[None, None, :]).astype(
        jnp.float32
    )
    ranks = jnp.sum(onehot * jnp.arange(bricks, dtype=jnp.float32)[None, :, None], axis=1)
    return (ranks[:, None, :] < ranks[:, :, None]).astype(jnp.float32)


def many_bricks(pressure, light, palette, rate, shear, offset, order):
    depth_cells, rows, cols = pressure.shape
    brick = lax.axis_index("gz")
    zero = jnp.zeros((), jnp.int32)
    widened = padded(pressure, (("gy", 1), ("gx", 2)), SHEAR + 1)
    slab = padded(widened, (("gz", 0),), 1)
    inner, normals = surface_terms(slab)
    shifts = lax.dynamic_slice(shear, (zero, brick * depth_cells, zero), (VIEWS, depth_cells, 2))
    layers = render_layers(inner, normals, shifts, light, palette, rate, rows, cols)
    moved = lax.dynamic_index_in_dim(offset, brick, 1, keepdims=False)
    blank = jnp.zeros((4, rows + REACH, cols + REACH), jnp.float32)
    canvas = jnp.stack(
        [
            lax.dynamic_update_slice(blank, layers[view], (zero, moved[view, 0], moved[view, 1]))
            for view in range(VIEWS)
        ]
    )
    own_tile = canvas[:, :, :rows, :cols]
    from_above = shifted(canvas[:, :, rows:, :cols], "gy", 1)
    from_left = shifted(canvas[:, :, :rows, cols:], "gx", 1)
    from_diagonal = shifted(canvas[:, :, rows:, cols:], ("gy", "gx"), lax.axis_size("gx") + 1)
    from_diagonal = from_diagonal * (lax.axis_index("gx") > 0).astype(jnp.float32)
    own_tile = own_tile.at[:, :, :REACH, :].add(from_above)
    own_tile = own_tile.at[:, :, :, :REACH].add(from_left)
    own_tile = own_tile.at[:, :, :REACH, :REACH].add(from_diagonal)
    ranking = precedence(order)
    pieces = lax.all_to_all(own_tile[None], "gz", split_axis=3, concat_axis=0, tiled=True)
    depths = pieces[:, :, 3]
    cover = jnp.einsum("vbc,cvyx->bvyx", ranking, depths, precision=lax.Precision.HIGHEST)
    colors = jnp.sum(pieces[:, :, :3] * jnp.exp(-cover)[:, :, None], axis=0)
    opacity = 1.0 - jnp.exp(-jnp.sum(depths, axis=0))
    image = jnp.concatenate([colors, opacity[:, None]], axis=1)
    return image[:, :, None]


def segments(tall):
    return (0, HALO, tall - HALO)


def exchange(
    dims, mine, here, p_ref, m_ref, full_in, rest_in, ends_in, full_out, rest_out, ends_out, sends,
    arrivals, local_sem,
):
    ny, nx, bz, rows = dims
    z, y, x = here
    strip = rows // 2
    tall = HALO + strip + SUB
    per = LANES // HALO
    groups = -(-bz // per)
    other = 1 - mine
    first_lane = LANES - HALO
    has_up, has_down = y > 0, y < ny - 1
    has_left, has_right = x > 0, x < nx - 1

    def remote(src, dst, slot, arrival, who):
        return pltpu.make_async_remote_copy(
            src_ref=src,
            dst_ref=dst,
            send_sem=sends.at[slot],
            recv_sem=arrivals.at[arrival],
            device_id=who,
            device_id_type=MESH,
        )

    def spans(to):
        if to == 0:
            return pl.ds(0, strip + SUB), pl.ds(HALO, strip + SUB)
        return pl.ds(strip - HALO, HALO + strip), pl.ds(0, HALO + strip)

    def main(brick, g):
        count = min(per, bz - g * per)
        source, target = spans(1 - brick)
        return remote(
            p_ref.at[pl.ds(g * per, count), source],
            m_ref.at[pl.ds(1 + brick * bz + g * per, count), target],
            g, g, (1 - z, y, x),
        )

    def down(brick):
        return remote(
            p_ref.at[:, pl.ds(rows - HALO, HALO)],
            m_ref.at[pl.ds(1 + brick * bz, bz), pl.ds(0, HALO)],
            groups, groups + brick, (0, y + 1, x),
        )

    def up(brick):
        return remote(
            p_ref.at[:, pl.ds(0, SUB)],
            m_ref.at[pl.ds(1 + brick * bz, bz), pl.ds(HALO + strip, SUB)],
            groups + 1, groups + brick, (1, y - 1, x),
        )

    def rightward(brick, g):
        slot = groups + 2 + brick * groups + g
        if g == groups - 1:
            return remote(rest_out.at[brick], rest_in.at[brick], slot, slot, (z, y, x + 1))
        at = brick * (groups - 1) + g
        return remote(full_out.at[at], full_in.at[at], slot, slot, (z, y, x + 1))

    def leftward(brick):
        slot = 3 * groups + 2 + brick
        return remote(ends_out.at[brick], ends_in.at[brick], slot, slot, (z, y, x - 1))

    def started(there, copy):
        @pl.when(there)
        def _():
            copy.start()

    def arrived(there, copy):
        @pl.when(there)
        def _():
            copy.wait_recv()

    def left(there, copy):
        @pl.when(there)
        def _():
            copy.wait_send()

    def pack(brick, g):
        if g == groups - 1:
            lane = lax.broadcasted_iota(jnp.int32, (HALO, LANES), 1)
            pieces = [m_ref[brick * bz + bz, row : row + HALO] for row in segments(tall)]
        else:
            lane = lax.broadcasted_iota(jnp.int32, (tall, LANES), 1)
            pieces = [m_ref[1 + brick * bz + g * per + j] for j in range(per)]
        packed = pltpu.roll(pieces[0], LANES - first_lane, 1)
        for j in range(1, per):
            moved = pltpu.roll(pieces[j], (j * HALO - first_lane) % LANES, 1)
            packed = jnp.where(lane >= j * HALO, moved, packed)
        if g == groups - 1:
            rest_out[brick] = packed
        else:
            full_out[brick * (groups - 1) + g] = packed

    def pack_ends(brick):
        lane = lax.broadcasted_iota(jnp.int32, (BLOCK, LANES), 1)
        ends = jnp.zeros((BLOCK, LANES), jnp.float32)
        for j in range(bz):
            for i in range(tall // BLOCK):
                at = i * bz + j
                cells = m_ref[1 + brick * bz + j, i * BLOCK : (i + 1) * BLOCK]
                ends = jnp.where(lane == at, pltpu.roll(cells, at, 1) if at else cells, ends)
        ends_out[brick] = ends

    def halo_in(brick):
        if mine == 0:
            arrived(has_up, down(brick))
        else:
            arrived(has_down, up(brick))

    def own():
        source, target = spans(mine)
        return pltpu.make_async_copy(
            p_ref.at[:, source], m_ref.at[pl.ds(1 + mine * bz, bz), target], local_sem
        )

    def open_up():
        for g in range(groups):
            main(mine, g).start()
        started(has_down, down(mine))
        started(has_up, up(mine))
        own().wait()
        halo_in(mine)
        for g in range(groups):
            pack(mine, g)
            started(has_right, rightward(mine, g))
        pack_ends(mine)
        started(has_left, leftward(mine))
        halo_in(other)
        for g in range(groups):
            main(other, g).wait_recv()
            pack(other, g)
            started(has_right, rightward(other, g))
        pack_ends(other)
        started(has_left, leftward(other))

    def columns_in(brick):
        for g in range(groups):
            arrived(has_left, rightward(brick, g))
        arrived(has_right, leftward(brick))

    def close():
        for g in range(groups):
            main(mine, g).wait_send()
        left(has_down, down(mine))
        left(has_up, up(mine))
        for brick in range(2):
            for g in range(groups):
                left(has_right, rightward(brick, g))
            left(has_left, leftward(brick))

    return open_up, columns_in, close, own


def render(
    dims, light_in, palette_in, rate_in, shear_in, offset_in, order_in, p_ref, out_ref,
    light, palette, rate, shear, offset, order, m_ref, full_in, rest_in, ends_in,
    full_out, rest_out, ends_out, h_ref, r_ref, dm, dh, sends, arrivals, local_sem, table_sems,
):
    ny, nx, bz, rows = dims
    strip = rows // 2
    tall = HALO + strip + SUB
    depth = 2 * bz
    per = LANES // HALO
    groups = -(-bz // per)
    first_lane = LANES - HALO
    z, y, x = lax.axis_index("gz"), lax.axis_index("gy"), lax.axis_index("gx")
    has_up, has_down = y > 0, y < ny - 1
    has_left, has_right = x > 0, x < nx - 1

    tables = [
        pltpu.make_async_copy(source, target, table_sems.at[i])
        for i, (source, target) in enumerate(
            (
                (light_in, light), (palette_in, palette), (rate_in, rate),
                (shear_in, shear), (offset_in, offset), (order_in, order),
            )
        )
    ]
    cross = y + 2 * z - 1
    partners = (
        (y >= 0, (1 - z, y, x)),
        (has_up, (z, y - 1, x)),
        (has_down, (z, y + 1, x)),
        (jnp.logical_and(cross >= 0, cross < ny), (1 - z, cross, x)),
        (has_left, (z, y, x - 1)),
        (has_right, (z, y, x + 1)),
    )
    barrier = pltpu.get_barrier_semaphore()
    count = 0
    for there, who in partners:

        @pl.when(there)
        def _():
            pl.semaphore_signal(barrier, inc=1, device_id=who, device_id_type=MESH)

        count = count + there.astype(jnp.int32)
    steps = [
        exchange(
            dims, mine, (z, y, x), p_ref, m_ref, full_in, rest_in, ends_in, full_out, rest_out,
            ends_out, sends, arrivals, local_sem,
        )
        for mine in range(2)
    ]

    for mine in range(2):

        @pl.when(z == mine)
        def _():
            steps[mine][3]().start()

    for copy in tables:
        copy.start()

    empty = jnp.zeros((tall, LANES), jnp.float32)
    for ref in (m_ref, h_ref):
        ref[0] = empty
        ref[depth + 1] = empty

    @pl.when(jnp.logical_and(z == 0, y == 0))
    def _():
        m_ref[:, :HALO] = jnp.zeros((depth + 2, HALO, LANES), jnp.float32)

    @pl.when(jnp.logical_and(z == 1, y == ny - 1))
    def _():
        m_ref[:, HALO + strip :] = jnp.zeros((depth + 2, SUB, LANES), jnp.float32)

    @pl.when(x == 0)
    def _():
        full_in[...] = jnp.zeros(full_in.shape, jnp.float32)
        rest_in[...] = jnp.zeros(rest_in.shape, jnp.float32)

    @pl.when(x == nx - 1)
    def _():
        ends_in[...] = jnp.zeros(ends_in.shape, jnp.float32)

    pl.semaphore_wait(barrier, count)

    for mine in range(2):

        @pl.when(z == mine)
        def _():
            steps[mine][0]()
            steps[mine][1](mine)

    def unpack(brick):
        for j in range(bz - 1):
            shift = (first_lane - (j % per) * HALO) % LANES
            cells = full_in[brick * (groups - 1) + j // per]
            h_ref[1 + brick * bz + j] = pltpu.roll(cells, shift, 1)
        cells = rest_in[brick]
        for j, row in enumerate(segments(tall)):
            moved = pltpu.roll(cells, (first_lane - j * HALO) % LANES, 1)
            h_ref[brick * bz + bz, row : row + HALO] = moved
        cells = ends_in[brick]
        for i in range(tall // BLOCK):
            moved = pltpu.roll(cells, (LANES - 1 - i * bz) % LANES, 1)
            r_ref[brick, i * BLOCK : (i + 1) * BLOCK] = moved

    for copy in tables:
        copy.wait()

    towards = []
    for w in range(VIEWS):
        a, b, c = light[w, 0], light[w, 1], light[w, 2]
        inverse = lax.rsqrt(jnp.full((SUB, LANES), a * a + b * b + c * c + 1.0, jnp.float32))
        towards.append((a * inverse, b * inverse, c * inverse))

    lane = lax.broadcasted_iota(jnp.int32, (SUB, LANES), 1)
    last = lane == LANES - 1
    first = lane == 0

    def slopes(k, carry):
        for i in range((HALO + strip) // SUB):
            top = i * SUB
            here = m_ref[k + 1, top + 1 : top + 1 + SUB]
            side = h_ref[k + 1, top + 1 : top + 1 + SUB]
            beyond = pltpu.roll(
                r_ref[k // bz, top + 1 : top + 1 + SUB], (LANES - k % bz) % LANES, 1
            )
            here_r, here_l = pltpu.roll(here, LANES - 1, 1), pltpu.roll(here, 1, 1)
            side_r, side_l = pltpu.roll(side, LANES - 1, 1), pltpu.roll(side, 1, 1)
            for ref, cols, dots in (
                (m_ref, jnp.where(last, beyond, here_r) - jnp.where(first, side_l, here_l), dm),
                (h_ref, jnp.where(last, here_r, side_r) - side_l, dh),
            ):
                deep = ref[k + 2, top + 1 : top + 1 + SUB] - ref[k, top + 1 : top + 1 + SUB]
                down = ref[k + 1, top + 2 : top + 2 + SUB] - ref[k + 1, top : top + SUB]
                half = 0.5 * lax.rsqrt(0.25 * (deep * deep + down * down + cols * cols) + 1.0)
                deep, down, cols = deep * half, down * half, cols * half
                for w in range(VIEWS):
                    a, b, c = towards[w]
                    dots[w, k, top : top + SUB] = deep * a + down * b + cols * c
        return carry

    unpack(z)
    lax.fori_loop(z * (bz + 1), z * (bz + 1) + bz - 1, slopes, 0)

    for mine in range(2):

        @pl.when(z == mine)
        def _():
            steps[mine][1](1 - mine)
            steps[mine][2]()

    unpack(1 - z)
    lax.fori_loop((1 - z) * (bz - 1), (1 - z) * (bz - 1) + bz + 1, slopes, 0)

    tile = 32
    base_row = y * rows + z * strip
    base_col = x * LANES
    lanes = lax.broadcasted_iota(jnp.int32, (tile, LANES), 1)
    rows_at = lax.broadcasted_iota(jnp.int32, (tile, LANES), 0)
    bias = [0.5 * palette[0, c] for c in range(3)]
    gain = [0.5 * palette[1, c] for c in range(3)]

    def view_part(step, carry):
        w = step // (strip // tile)
        top = (step % (strip // tile)) * tile
        through = jnp.ones((tile, LANES), jnp.float32)
        ambient = jnp.zeros((tile, LANES), jnp.float32)
        colors = [jnp.zeros((tile, LANES), jnp.float32) for _ in range(3)]
        rate2 = rate[w] * (-math.log2(math.e))
        for place in range(2):
            brick = order[place, w]
            off_r, off_c = offset[brick, 0, w], offset[brick, 1, w]
            inside = jnp.logical_and(
                rows_at >= off_r - base_row - top, lanes >= off_c - base_col
            )
            fall = jnp.where(inside, rate2, 0.0)
            for j in range(bz):
                k = brick * bz + j
                sr = off_r + shear[w, 0, k]
                sc = off_c + shear[w, 1, k]
                at = HALO + top - sr
                wrap = lanes >= LANES - sc
                value = jnp.where(
                    wrap, h_ref[k + 1, pl.ds(at, tile)], m_ref[k + 1, pl.ds(at, tile)]
                )
                dot = jnp.where(wrap, dh[w, k, pl.ds(at - 1, tile)], dm[w, k, pl.ds(at - 1, tile)])
                value = pltpu.roll(value, sc, 1)
                dot = pltpu.roll(dot, sc, 1)
                kept = jnp.exp2(fall * (1.0 + jnp.tanh(value)))
                weight = (0.125 + 0.375 * dot * dot) * ((1.0 - kept) * through)
                through = through * kept
                ambient = ambient + weight
                for c in range(3):
                    colors[c] = colors[c] + weight * jnp.tanh(bias[c] + gain[c] * value)
        for c in range(3):
            out_ref[w, c, pl.ds(top, tile)] = ambient + colors[c]
        out_ref[w, 3, pl.ds(top, tile)] = 1.0 - through
        return carry

    lax.fori_loop(0, VIEWS * (strip // tile), view_part, 0)


def two_bricks(mesh, pressure, light, palette, rate, shear, offset, order):
    bz, rows, cols = pressure.shape
    dims = (mesh.shape["gy"], mesh.shape["gx"], bz, rows)
    strip = rows // 2
    tall = HALO + strip + SUB
    depth = 2 * bz
    groups = -(-bz // (LANES // HALO))
    vmem = pl.BlockSpec(memory_space=pltpu.VMEM)
    hbm = pl.BlockSpec(memory_space=pltpu.HBM)
    f32 = jnp.float32
    copies = 3 * groups + 4
    tables = (
        light,
        palette.T,
        rate,
        jnp.transpose(shear, (0, 2, 1)),
        jnp.transpose(offset, (1, 2, 0)),
        order.T,
    )
    image = pl.pallas_call(
        functools.partial(render, dims),
        out_shape=jax.ShapeDtypeStruct((VIEWS, 4, strip, LANES), f32),
        in_specs=[hbm] * 7,
        out_specs=vmem,
        scratch_shapes=[
            *[pltpu.SMEM(table.shape, table.dtype) for table in tables],
            pltpu.VMEM((depth + 2, tall, LANES), f32),
            pltpu.VMEM((2 * groups - 2, tall, LANES), f32),
            pltpu.VMEM((2, HALO, LANES), f32),
            pltpu.VMEM((2, BLOCK, LANES), f32),
            pltpu.VMEM((2 * groups - 2, tall, LANES), f32),
            pltpu.VMEM((2, HALO, LANES), f32),
            pltpu.VMEM((2, BLOCK, LANES), f32),
            pltpu.VMEM((depth + 2, tall, LANES), f32),
            pltpu.VMEM((2, tall, LANES), f32),
            pltpu.VMEM((VIEWS, depth, HALO + strip, LANES), f32),
            pltpu.VMEM((VIEWS, depth, HALO + strip, LANES), f32),
            pltpu.SemaphoreType.DMA((copies,)),
            pltpu.SemaphoreType.DMA((copies,)),
            pltpu.SemaphoreType.DMA,
            pltpu.SemaphoreType.DMA((len(tables),)),
        ],
        compiler_params=pltpu.CompilerParams(collective_id=0, has_side_effects=True, vmem_limit_bytes=12 << 20),
        name="render",
    )(
        *[pltpu.with_memory_space_constraint(t, pltpu.HBM) for t in (*tables, pressure)]
    )
    return image[:, :, None]


def fits(mesh, shape):
    bz, rows, cols = shape
    tall = HALO + rows // 2 + SUB
    return (
        mesh.shape["gz"] == 2
        and cols == LANES
        and rows % 64 == 0
        and 2 * HALO <= tall <= 3 * HALO
        and tall % BLOCK == 0
        and bz % (LANES // HALO) == 1
        and bz * (tall // BLOCK) <= LANES
    )


def on_device(mesh, pressure, *rest):
    if fits(mesh, pressure.shape):
        return two_bricks(mesh, pressure, *rest)
    return many_bricks(pressure, *rest)


def solution(mesh):
    return jax.shard_map(
        functools.partial(on_device, mesh),
        mesh=mesh,
        in_specs=(P("gz", "gy", "gx"), P(), P(), P(), P(), P(), P()),
        out_specs=P(None, None, "gz", "gy", "gx"),
        check_vma=False,
    )
```
